128 devices in a mesh: seq: 4 (over z_lo, core), blk: 32 (over y, x, z_hi).
Axes of the slice: x: 4, y: 4, z: 4 (z_hi: 2, z_lo: 2; z = z_hi * 2 + z_lo), core: 2. Of those that a mesh axis runs over, the one named last changes fastest.
Arguments:
- patches: bfloat16 [32768, 1280], P(('seq', 'blk')), may hold values from -40 to 40
- vis_gain: float32 [1280], replicated, may hold values from 0.1 to 1.9
- vis_up: bfloat16 [5120, 1280], P('seq'), may hold values from -0.15625 to 0.15625
- vis_bias: float32 [5120], P('seq'), may hold values from -4 to 4
- vis_down: bfloat16 [5120, 1280], P('seq'), may hold values from -0.078125 to 0.078125
- merge_gain: float32 [1280], replicated, may hold values from 0.1 to 1.9
- merge_proj: bfloat16 [5120, 1280], replicated, may hold values from -0.078125 to 0.078125
- text_embed: bfloat16 [16384, 1280], P(('seq', 'blk')), may hold values from -40 to 40
- slot_index: int32 [8192], P(('seq', 'blk')), may hold values from 0 to 16383, as said below
- text_gain: float32 [1280], replicated, may hold values from 0.1 to 1.9
- text_up: bfloat16 [5120, 1280], P('blk'), may hold values from -0.15625 to 0.15625
- text_down: bfloat16 [5120, 1280], P('blk'), may hold values from -0.078125 to 0.078125
Outputs:
- hidden_out: bfloat16 [16384, 1280], P(('seq', 'blk'))
The draws below stay inside these ranges and needn't reach their ends.
Inputs may be any that keep to these rules, and one draw needn't show every extreme that they name: slot_index values are distinct. The merged rows held by one device go to prompt tokens held by devices with the same seq index. Each device sends either no merged rows or exactly 4 merged rows to each device of its blk group; in every draw some device receives 4 rows from every device of its blk group.
All inputs are finite; a program needn't handle non-finite values.
Results may differ from the reference program's by a relative error of at most 0.015.
Values may be sent and summed in bfloat16 or wider, within the bound.
A program may use at most 192 MiB of HBM per device.

```python
import math
import jax
import jax.numpy as jnp
from jax import lax

D = 1280
FF = 5120
TFF = 5120
MD = 5120
P_DEV = 256
T_DEV = 128
M_DEV = 64
CAP = 4
PATCHES = 32768
MERGED = 8192
TOKENS = 16384


def scaled_rows(key, row_total, col_total):
    key_base, key_rows, key_cols = jax.random.split(key, 3)
    base = jnp.clip(jax.random.normal(key_base, (row_total, col_total), jnp.float32), -4.0, 4.0)
    row_scale = jnp.exp(jax.random.uniform(key_rows, (row_total, 1), jnp.float32, math.log(0.3), math.log(3.0)))
    col_scale = jnp.exp(jax.random.uniform(key_cols, (1, col_total), jnp.float32, math.log(0.3), math.log(3.0)))
    return (base * row_scale * col_scale).astype(jnp.bfloat16)


def draw_patches(key, part):
    return scaled_rows(jax.random.fold_in(key, 11), PATCHES, D)


def draw_text_embed(key, part):
    return scaled_rows(jax.random.fold_in(key, 12), TOKENS, D)


def draw_slot_index(key, part):
    cycle_size = 2 * M_DEV // CAP
    window = cycle_size // 2
    group_total = TOKENS // (T_DEV * cycle_size)

    def one_group(group_key, group_number):
        key_base, key_start, key_perm = jax.random.split(group_key, 3)
        centre = jax.random.randint(key_base, (), 0, cycle_size)
        starts = (centre - jax.random.randint(key_start, (cycle_size,), 0, window)) % cycle_size
        steps_in = jnp.arange(window, dtype=jnp.int32)
        targets = (starts[:, None] + steps_in[None, :]) % cycle_size
        devices = jnp.arange(cycle_size, dtype=jnp.int32)
        covers = ((devices[None, :] - starts[:, None]) % cycle_size < window).astype(jnp.int32)
        before = jnp.cumsum(covers, axis=0) - covers
        orders = jax.vmap(lambda perm_key: jax.random.permutation(perm_key, T_DEV).astype(jnp.int32))(jax.random.split(key_perm, cycle_size))
        sources = jnp.arange(cycle_size, dtype=jnp.int32)[:, None, None]
        within = jnp.arange(CAP, dtype=jnp.int32)[None, None, :]
        target_full = targets[:, :, None]
        ranks = CAP * before[sources, target_full] + within
        position = orders[target_full, ranks]
        slots = group_number * cycle_size * T_DEV + target_full * T_DEV + position
        return slots.reshape(cycle_size * M_DEV).astype(jnp.int32)
    keys_all = jax.random.split(jax.random.fold_in(key, 13), group_total)
    numbers = jnp.arange(group_total, dtype=jnp.int32)
    return jax.vmap(one_group)(keys_all, numbers).reshape(MERGED).astype(jnp.int32)


def block_levels(stream_key, shape, pieces, least, high):
    factor_of, own = 1.0, jax.random.fold_in(stream_key, 6)
    for dim, blocks in pieces:
        heights = jnp.exp(jax.random.uniform(jax.random.fold_in(own, dim), (blocks,), jnp.float32, least / len(pieces), high / len(pieces)))
        factor_of = factor_of * jnp.repeat(heights, shape[dim] // blocks).reshape([-1 if axis == dim else 1 for axis in range(len(shape))])
    return factor_of


def bell_draw(stream_key, dims, scale, limit, cuts=(), held_as=jnp.bfloat16):
    factor_of = block_levels(stream_key, dims, cuts, -0.22, 0.18) if cuts else 1.0
    result = jax.random.normal(stream_key, dims, jnp.float32) * scale * factor_of
    return jnp.minimum(jnp.maximum(result, -limit), limit).astype(held_as)


def setup_inputs(seed: int = 0) -> dict:
    keys = jax.random.split(jax.random.key(seed), 13)
    return {
        "patches": draw_patches(jax.random.fold_in(keys[12], 71), 0),
        "vis_gain": jnp.clip(1.0 + 0.18 * jax.random.normal(keys[1], (D,), jnp.float32), 0.1, 1.9),
        "vis_up": bell_draw(keys[2], (FF, D), D ** -0.5, 0.15625, ((0, 4),)),
        "vis_bias": bell_draw(keys[3], (FF,), 1.0, 4.0, ((0, 4),), jnp.float32),
        "vis_down": bell_draw(keys[4], (FF, D), FF ** -0.5, 0.078125, ((0, 4),)),
        "merge_gain": jnp.clip(1.0 + 0.18 * jax.random.normal(keys[5], (D,), jnp.float32), 0.1, 1.9),
        "merge_proj": bell_draw(keys[6], (MD, D), MD ** -0.5, 0.078125),
        "text_embed": draw_text_embed(jax.random.fold_in(keys[12], 71), 0),
        "slot_index": draw_slot_index(jax.random.fold_in(keys[12], 71), 0),
        "text_gain": jnp.clip(1.0 + 0.18 * jax.random.normal(keys[9], (D,), jnp.float32), 0.1, 1.9),
        "text_up": bell_draw(keys[10], (TFF, D), D ** -0.5, 0.15625, ((0, 32),)),
        "text_down": bell_draw(keys[11], (TFF, D), TFF ** -0.5, 0.078125, ((0, 32),)),
    }


def normalize(values, row_gain):
    values = values.astype(jnp.float32)
    center = values - lax.optimization_barrier(jnp.mean(values, axis=-1, keepdims=True))
    spread = lax.optimization_barrier(jnp.mean(center * center, axis=-1, keepdims=True))
    return center * lax.rsqrt(spread + 1e-06) * row_gain

def vision_block(rows_in, vis_gain, vis_up, vis_bias, vis_down, merge_gain, merge_proj):
    normed = normalize(rows_in, vis_gain).astype(jnp.bfloat16)
    pre_act = jnp.dot(normed, vis_up.T, preferred_element_type=jnp.float32) + vis_bias
    hidden = jax.nn.gelu(pre_act, approximate=True).astype(jnp.bfloat16)
    vis_out = rows_in.astype(jnp.float32) + jnp.dot(hidden, vis_down, preferred_element_type=jnp.float32)
    merge_normed = normalize(vis_out, merge_gain).astype(jnp.bfloat16)
    joined = merge_normed.reshape(merge_normed.shape[0] // 4, 4 * merge_normed.shape[1])
    return jnp.dot(joined, merge_proj, preferred_element_type=jnp.float32).astype(jnp.bfloat16)

def text_block(rows_in, text_gain, text_up, text_down):
    normed = normalize(rows_in, text_gain).astype(jnp.bfloat16)
    hidden = jax.nn.gelu(jnp.dot(normed, text_up.T, preferred_element_type=jnp.float32), approximate=True).astype(jnp.bfloat16)
    summed = rows_in.astype(jnp.float32) + jnp.dot(hidden, text_down, preferred_element_type=jnp.float32)
    return summed.astype(jnp.bfloat16)

def reference(patches, vis_gain, vis_up, vis_bias, vis_down, merge_gain, merge_proj, text_embed, slot_index, text_gain, text_up, text_down):
    stacked = patches.reshape(PATCHES // P_DEV, P_DEV, D)
    merged = lax.map(lambda rows_in: vision_block(rows_in, vis_gain, vis_up, vis_bias, vis_down, merge_gain, merge_proj), stacked)
    merged = merged.reshape(MERGED, D)
    text_rows = text_embed.at[slot_index].set(merged)
    outputs = lax.map(lambda rows_in: text_block(rows_in, text_gain, text_up, text_down), text_rows.reshape(TOKENS // T_DEV, T_DEV, D))
    return outputs.reshape(TOKENS, D)
```

```python
import jax
import jax.numpy as jnp
from jax import lax
from jax.sharding import PartitionSpec as P


def normalize(values, row_gain):
    values = values.astype(jnp.float32)
    center = values - jnp.mean(values, axis=-1, keepdims=True)
    spread = jnp.mean(center * center, axis=-1, keepdims=True)
    return center * lax.rsqrt(spread + 1e-06) * row_gain


def up_project(rows_in, up_piece):
    return lax.dot_general(
        rows_in, up_piece, (((1,), (1,)), ((), ())), preferred_element_type=jnp.float32
    )


def before(mask):
    size = mask.shape[1]
    ahead = (jnp.arange(size)[:, None] < jnp.arange(size)[None, :]).astype(jnp.bfloat16)
    return jnp.dot(
        mask.astype(jnp.bfloat16), ahead, preferred_element_type=jnp.float32
    ).astype(jnp.int32)


def per_device(
    patches,
    vis_gain,
    vis_up,
    vis_bias,
    vis_down,
    merge_gain,
    merge_proj,
    text_embed,
    slot_index,
    text_gain,
    text_up,
    text_down,
):
    rows_here, width = patches.shape
    seq_size, cycle_size = lax.axis_size("seq"), lax.axis_size("blk")
    seq, blk = lax.axis_index("seq"), lax.axis_index("blk")
    token_count = text_embed.shape[0]
    merged_count = slot_index.shape[0]
    capacity = 2 * merged_count // cycle_size

    piece = text_up.shape[0] // seq_size
    mine = jnp.concatenate(
        [
            lax.dynamic_slice_in_dim(text_up, seq * piece, piece, 0),
            lax.dynamic_slice_in_dim(text_down, seq * piece, piece, 0),
        ],
        axis=0,
    )
    weights = lax.all_gather(mine, "blk", axis=0)
    all_slots = lax.all_gather(slot_index, "blk", axis=0)

    vis_normed = normalize(patches, vis_gain).astype(jnp.bfloat16)
    gathered = lax.all_gather(vis_normed, "seq", axis=0, tiled=True)
    hidden = jax.nn.gelu(up_project(gathered, vis_up) + vis_bias, approximate=True).astype(
        jnp.bfloat16
    )
    vis_mlp = lax.psum_scatter(
        jnp.dot(hidden, vis_down, preferred_element_type=jnp.float32).astype(jnp.bfloat16),
        "seq",
        scatter_dimension=0,
        tiled=True,
    ).astype(jnp.float32)
    vis_out = patches.astype(jnp.float32) + vis_mlp
    merge_normed = normalize(vis_out, merge_gain).astype(jnp.bfloat16)
    joined = merge_normed.reshape(rows_here // 4, 4 * width)
    merged = jnp.dot(joined, merge_proj, preferred_element_type=jnp.float32).astype(jnp.bfloat16)

    target = slot_index // token_count % cycle_size
    to_target = jnp.arange(cycle_size, dtype=jnp.int32)[:, None] == target[None, :]
    rank = jnp.sum(jnp.where(to_target, before(to_target), 0), axis=0)
    slot = target * capacity + rank
    pick = (jnp.arange(cycle_size * capacity)[:, None] == slot[None, :]).astype(jnp.bfloat16)
    send_rows = jnp.dot(pick, merged, preferred_element_type=jnp.float32).astype(jnp.bfloat16)
    got_rows = lax.all_to_all(send_rows, "blk", split_axis=0, concat_axis=0, tiled=True)

    for_me = (all_slots // token_count % cycle_size) == blk
    rank_in = before(for_me)
    chosen = for_me[:, None, :] & (
        rank_in[:, None, :] == jnp.arange(capacity, dtype=jnp.int32)[None, :, None]
    )
    where = jnp.sum(jnp.where(chosen, (all_slots % token_count)[:, None, :] + 1, 0), axis=2) - 1
    place = jnp.arange(token_count, dtype=jnp.int32)[:, None] == where.reshape(1, -1)
    placed = jnp.dot(
        place.astype(jnp.bfloat16), got_rows, preferred_element_type=jnp.float32
    ).astype(jnp.bfloat16)
    text_rows = jnp.where(jnp.any(place, axis=1, keepdims=True), placed, text_embed)

    text_normed = normalize(text_rows, text_gain).astype(jnp.bfloat16)
    gathered_tokens = lax.all_gather(text_normed, "seq", axis=0, tiled=True)
    up_part = weights[:, :piece].reshape(-1, width)
    down_part = weights[:, piece:].reshape(-1, width)
    hidden = jax.nn.gelu(up_project(gathered_tokens, up_part), approximate=True).astype(
        jnp.bfloat16
    )
    text_mlp = lax.psum_scatter(
        jnp.dot(hidden, down_part, preferred_element_type=jnp.float32).astype(jnp.bfloat16),
        "seq",
        scatter_dimension=0,
        tiled=True,
    ).astype(jnp.float32)
    return (text_rows.astype(jnp.float32) + text_mlp).astype(jnp.bfloat16)


def solution(mesh):
    placed = (
        P(("seq", "blk"), None),
        P(),
        P("seq", None),
        P("seq"),
        P("seq", None),
        P(),
        P(),
        P(("seq", "blk"), None),
        P(("seq", "blk")),
        P(),
        P("blk", None),
        P("blk", None),
    )
    return jax.shard_map(
        per_device, mesh=mesh, in_specs=placed, out_specs=P(("seq", "blk"), None), check_vma=False
    )
```

```python
import functools

import jax
import jax.numpy as jnp
from jax import lax
from jax.experimental import pallas as pl
from jax.experimental.pallas import tpu as pltpu
from jax.sharding import PartitionSpec as P

MESH = pl.DeviceIdType.MESH
D = 1280
ROWS = 256
TOK = 128
QUARTER = 1280
HALF = 2 * QUARTER
BLK = 32
CAP = 4
PIECE = 80
COLS = 256
NCOL = D // COLS
PART = 128

S_VROW, S_UP, S_BIAS, S_DOWN, S_VBACK = 0, 2, 3, 4, 9
S_SLOT, S_A2A, S_TROW, S_TBACK = 19, 20, 21, 22
S_OX, S_QZ, S_QY, S_OY, S_QX, S_PAIR = 27, 30, 31, 34, 37, 40
N_SEM = 48


def normalize(values, row_gain):
    center = values - jnp.mean(values, axis=-1, keepdims=True)
    spread = jnp.mean(center * center, axis=-1, keepdims=True)
    return center * lax.rsqrt(spread + 1e-06) * row_gain


def gelu(v):
    return jax.nn.gelu(v, approximate=True)


def dot(a, b):
    return jnp.dot(a, b, preferred_element_type=jnp.float32)


def dot_t(a, b):
    return lax.dot_general(a, b, (((1,), (1,)), ((), ())), preferred_element_type=jnp.float32)


def before(mask):
    size = mask.shape[1]
    ahead = lax.broadcasted_iota(jnp.int32, (size, size), 0) < lax.broadcasted_iota(
        jnp.int32, (size, size), 1
    )
    ones = jnp.where(mask, 1.0, 0.0).astype(jnp.bfloat16)
    return dot(ones, jnp.where(ahead, 1.0, 0.0).astype(jnp.bfloat16)).astype(jnp.int32)


def step(
    patches,
    small,
    slots,
    vis_up,
    bias,
    vis_down,
    merge_proj,
    text_embed,
    text_up,
    text_down,
    out,
    rows_v,
    small_v,
    bias_v,
    x,
    hidden,
    up,
    down,
    proj,
    back_out,
    back_in,
    own,
    normed,
    joined,
    merged,
    send_rows,
    got_rows,
    got_f32,
    all_slots,
    embed_v,
    text_rows,
    text_w,
    tback_out,
    tback_in,
    send_sem,
    recv_sem,
    local_sem,
):
    seq, blk = lax.axis_index("seq"), lax.axis_index("blk")
    core, half = seq % 2, seq // 2
    px, py, pz = (blk // 2) % 4, blk // 8, (blk % 2) * 2 + half

    def place(cx, cy, cz, cc):
        cx, cy, cz = (cx + 4) % 4, (cy + 4) % 4, (cz + 4) % 4
        return ((cz % 2) * 2 + cc, (cy * 4 + cx) * 2 + cz // 2)

    twin = place(px, py, pz, 1 - core)
    partner = place(px, py, pz + 1 - 2 * core, 1 - core)
    other_hi = place(px, py, pz - 1 + 2 * half, core)
    along_x = [place(px + d, py, pz, core) for d in (1, -1, 2)]
    along_y = [place(px, py + d, pz, core) for d in (1, -1, 2)]

    def remote(src, dst, k, to):
        return pltpu.make_async_remote_copy(
            src_ref=src,
            dst_ref=dst,
            send_sem=send_sem.at[k],
            recv_sem=recv_sem.at[k],
            device_id=to,
            device_id_type=MESH,
        )

    def local(src, dst, k):
        return pltpu.make_async_copy(src, dst, local_sem.at[k])

    gate = pltpu.get_barrier_semaphore()

    def greet(i, carry):
        pl.semaphore_signal(
            gate, inc=1, device_id=(seq, (blk + i) % BLK), device_id_type=MESH
        )
        return carry

    for to in (twin, partner, other_hi):
        pl.semaphore_signal(gate, inc=1, device_id=to, device_id_type=MESH)
    lax.fori_loop(1, BLK, greet, 0)

    loads = [
        local(patches, rows_v, 0),
        local(small, small_v, 1),
        local(vis_up, up.at[pl.ds(0, QUARTER)], 2),
        local(bias, bias_v.at[0], 3),
        local(vis_down, down.at[pl.ds(0, QUARTER)], 4),
        local(slots, all_slots.at[blk], 5),
        local(text_embed, embed_v, 6),
        local(merge_proj, proj, 7),
    ]
    for copy in loads[:7]:
        copy.start()
    pl.semaphore_wait(gate, BLK + 2)

    twin_up = remote(vis_up, up.at[pl.ds(QUARTER, QUARTER)], S_UP, twin)
    twin_bias = remote(bias, bias_v.at[1], S_BIAS, twin)
    twin_up.start()
    twin_bias.start()
    loads[0].wait()
    loads[1].wait()

    row_copies = []
    for part in range(2):
        rows = pl.ds(part * PART, PART)
        v = rows_v[rows, :].astype(jnp.float32)
        x[pl.ds(ROWS + part * PART, PART), :] = normalize(v, small_v[0:1, :]).astype(jnp.bfloat16)
        copy = remote(x.at[pl.ds(ROWS + part * PART, PART)], x.at[rows], S_VROW + part, partner)
        copy.start()
        row_copies.append(copy)

    o_at = pl.ds(pl.multiple_of(PIECE * (4 * py + px), 16), PIECE)
    q_at = pl.ds(pl.multiple_of(HALF // 2 + PIECE * (4 * px + py), 16), PIECE)
    mine = pl.ds(pl.multiple_of(PIECE * half, 16), PIECE)
    theirs = pl.ds(pl.multiple_of(PIECE * (1 - half), 16), PIECE)
    q_out = lambda src: remote(src, text_w.at[core, q_at], S_QZ, other_hi)
    o_out = lambda src: [
        remote(src, text_w.at[core, o_at], S_OX + i, to) for i, to in enumerate(along_x)
    ]
    for which, source in ((0, text_up), (1, text_down)):

        @pl.when(core == which)
        def _():
            q_out(source.at[theirs]).start()
            local(source.at[mine], text_w.at[core, o_at], 8).start()
            for copy in o_out(source.at[mine]):
                copy.start()

    def tell(i, carry):
        remote(slots, all_slots.at[blk], S_SLOT, (seq, (blk + i) % BLK)).start()
        return carry

    lax.fori_loop(1, BLK, tell, 0)

    twin_down = [
        remote(
            vis_down.at[:, pl.ds(j * COLS, COLS)],
            down.at[pl.ds(QUARTER, QUARTER), pl.ds(j * COLS, COLS)],
            S_DOWN + j,
            twin,
        )
        for j in range(NCOL)
    ]
    for copy in twin_down:
        copy.start()
    loads[7].start()

    def up_block(rows, count, quarter):
        def body(j, carry):
            at = pl.multiple_of(j * COLS, COLS)
            h = dot_t(x[rows, :], up[pl.ds(quarter * QUARTER + at, COLS), :])
            h = h + bias_v[quarter, :, pl.ds(at, COLS)]
            hidden[rows, pl.ds(quarter * QUARTER + at, COLS)] = gelu(h).astype(jnp.bfloat16)
            return carry

        lax.fori_loop(0, NCOL, body, 0, unroll=True)

    own_rows = pl.ds(ROWS, ROWS)
    loads[2].wait()
    loads[3].wait()
    up_block(own_rows, ROWS, 0)

    q_copies = [
        remote(text_w.at[core, q_at], text_w.at[core, q_at], S_QY + i, to)
        for i, to in enumerate(along_y)
    ]
    q_out(text_w.at[core, q_at]).wait_recv()
    for copy in q_copies:
        copy.start()

    back_copies = []
    for part in range(2):
        rows = pl.ds(part * PART, PART)
        row_copies[part].wait_recv()
        up_block(rows, PART, 0)
        if part == 0:
            twin_up.wait_recv()
            twin_bias.wait_recv()
            loads[4].wait()
        up_block(rows, PART, 1)
        if part == 0:
            local(text_w.at[core, o_at], text_w.at[core, o_at], 8).wait()
            for copy in o_out(text_w.at[core, o_at]):
                copy.wait_recv()
            oy_at = pl.ds(pl.multiple_of(4 * PIECE * py, 16), 4 * PIECE)
            oy_copies = [
                remote(text_w.at[core, oy_at], text_w.at[core, oy_at], S_OY + i, to)
                for i, to in enumerate(along_y)
            ]
            for copy in oy_copies:
                copy.start()
        for j in range(NCOL):
            if part == 0:
                twin_down[j].wait_recv()
            cols = pl.ds(j * COLS, COLS)
            back_out[part, j] = dot(hidden[rows, :], down[:, cols]).astype(jnp.bfloat16)
            copy = remote(
                back_out.at[part, j], back_in.at[part, j], S_VBACK + part * NCOL + j, partner
            )
            copy.start()
            back_copies.append(copy)
        if part == 0:
            for copy in q_copies:
                copy.wait_recv()
            qx_at = pl.ds(pl.multiple_of(HALF // 2 + 4 * PIECE * px, 16), 4 * PIECE)
            qx_copies = [
                remote(text_w.at[core, qx_at], text_w.at[core, qx_at], S_QX + i, to)
                for i, to in enumerate(along_x)
            ]
            for copy in qx_copies:
                copy.start()

    pair_copies = []

    def pair_up(at):
        copy = remote(text_w.at[core, at], text_w.at[core, at], S_PAIR + len(pair_copies), twin)
        copy.start()
        pair_copies.append(copy)

    pair_up(oy_at)
    pair_up(qx_at)
    up_block(own_rows, ROWS, 1)
    for j in range(NCOL):
        cols = pl.ds(j * COLS, COLS)
        own[:, cols] = dot(hidden[own_rows, :], down[:, cols])

    remote(
        all_slots.at[pl.ds(0, BLK - 1)], all_slots.at[pl.ds(0, BLK - 1)], S_SLOT, twin
    ).wait()
    loads[5].wait()
    slot_rows = all_slots[:, 0, :]
    my_slots = all_slots[blk]
    target = (my_slots >> 7) % BLK
    to_target = lax.broadcasted_iota(jnp.int32, (BLK, 128), 0) == target
    to_target = to_target & (my_slots >= 0)
    rank = jnp.sum(jnp.where(to_target, before(to_target), 0), axis=0, keepdims=True)
    goes = jnp.where(my_slots >= 0, target * CAP + rank, -1)
    pick = lax.broadcasted_iota(jnp.int32, (BLK * CAP, 128), 0) == goes
    pick = jnp.where(pick, 1.0, 0.0).astype(jnp.bfloat16)[:, :64]

    for_me = ((slot_rows >> 7) % BLK == blk) & (slot_rows >= 0)
    rank_in = before(for_me)
    position = jnp.where(for_me, (slot_rows & (TOK - 1)) + 1, 0)
    lane = lax.broadcasted_iota(jnp.int32, (BLK, BLK * CAP), 1)
    source = lax.broadcasted_iota(jnp.int32, (BLK, BLK * CAP), 0)
    where = jnp.zeros((BLK, BLK * CAP), jnp.int32)
    for r in range(CAP):
        found = jnp.sum(jnp.where(rank_in == r, position, 0), axis=1, keepdims=True)
        where = where + jnp.where(lane == source * CAP + r, found, 0)
    where = jnp.sum(where, axis=0, keepdims=True) - 1
    placing = lax.broadcasted_iota(jnp.int32, (TOK, BLK * CAP), 0) == where
    placing = jnp.where(placing, 1.0, 0.0)

    for part in range(2):
        rows = pl.ds(part * PART, PART)
        for j in range(NCOL):
            back_copies[part * NCOL + j].wait_recv()
            cols = pl.ds(j * COLS, COLS)
            own[rows, cols] = (
                own[rows, cols]
                + back_in[part, j].astype(jnp.float32)
                + rows_v[rows, cols].astype(jnp.float32)
            )
        normed[rows, :] = normalize(own[rows, :], small_v[1:2, :]).astype(jnp.bfloat16)
    to_row = lax.broadcasted_iota(jnp.int32, (ROWS, ROWS), 0)
    from_row = lax.broadcasted_iota(jnp.int32, (ROWS, ROWS), 1)
    order = from_row == 4 * (to_row & 63) + (to_row >> 6)
    order = jnp.where(order, 1.0, 0.0).astype(jnp.bfloat16)
    for j in range(NCOL):
        moved = dot(order, normed[:, pl.ds(j * COLS, COLS)]).astype(jnp.bfloat16)
        for k in range(4):
            joined[:, pl.ds(k * D + j * COLS, COLS)] = moved[k * 64 : (k + 1) * 64, :]
    loads[7].wait()
    for j in range(NCOL):
        cols = pl.ds(j * COLS, COLS)
        merged[:, cols] = dot(joined[...], proj[:, cols]).astype(jnp.bfloat16)
    spread_rows = dot(pick, merged[...])
    for t in range(BLK):
        send_rows[t] = spread_rows[t * CAP : (t + 1) * CAP, :].astype(jnp.bfloat16)

    def send(i, carry):
        to = (blk + i) % BLK
        remote(send_rows.at[to], got_rows.at[blk], S_A2A, (seq, to)).start()
        return carry

    lax.fori_loop(1, BLK, send, 0)
    got_rows[blk] = send_rows[blk]

    for copies, base, coord in ((oy_copies, 0, py), (qx_copies, HALF // 2, px)):
        for i, d in enumerate((1, -1, 2)):
            copies[i].wait_recv()
            came = (coord - d + 4) % 4
            pair_up(pl.ds(pl.multiple_of(base + 4 * PIECE * came, 16), 4 * PIECE))

    remote(
        send_rows.at[pl.ds(0, BLK - 1)], got_rows.at[pl.ds(0, BLK - 1)], S_A2A, twin
    ).wait()
    for t in range(BLK):
        got_f32[pl.ds(t * CAP, CAP), :] = got_rows[t].astype(jnp.float32)
    loads[6].wait()
    placed = dot(placing.astype(jnp.bfloat16), got_f32[...].astype(jnp.bfloat16))
    filled = jnp.sum(placing, axis=1, keepdims=True) > 0.5
    text_rows[...] = jnp.where(filled, placed, embed_v[...].astype(jnp.float32))

    own_tok = pl.ds(TOK, TOK)
    x[own_tok, :] = normalize(text_rows[...], small_v[2:3, :]).astype(jnp.bfloat16)
    text_row = remote(x.at[own_tok], x.at[pl.ds(0, TOK)], S_TROW, partner)
    text_row.start()
    for copy in pair_copies:
        copy.wait_recv()

    def text_up_block(rows):
        def body(j, carry):
            at = pl.multiple_of(j * COLS, COLS)
            h = dot_t(x[rows, :], text_w[0, pl.ds(at, COLS), :])
            hidden[rows, pl.ds(at, COLS)] = gelu(h).astype(jnp.bfloat16)
            return carry

        lax.fori_loop(0, HALF // COLS, body, 0, unroll=True)

    text_up_block(own_tok)
    text_row.wait_recv()
    rows = pl.ds(0, TOK)
    text_up_block(rows)
    tback = []
    for j in range(NCOL):
        cols = pl.ds(j * COLS, COLS)
        tback_out[j] = dot(hidden[rows, :], text_w[1, :, cols]).astype(jnp.bfloat16)
        copy = remote(tback_out.at[j], tback_in.at[j], S_TBACK + j, partner)
        copy.start()
        tback.append(copy)
    for j in range(NCOL):
        cols = pl.ds(j * COLS, COLS)
        text_rows[:, cols] = text_rows[:, cols] + dot(hidden[own_tok, :], text_w[1, :, cols])
    for j in range(NCOL):
        cols = pl.ds(j * COLS, COLS)
        tback[j].wait_recv()
        out[:, cols] = (text_rows[:, cols] + tback_in[j].astype(jnp.float32)).astype(jnp.bfloat16)

    q_out(text_w.at[core, q_at]).wait_send()
    for copy in (
        o_out(text_w.at[core, o_at])
        + row_copies
        + [twin_up, twin_bias, text_row]
        + twin_down
        + back_copies
        + q_copies
        + oy_copies
        + qx_copies
        + pair_copies
        + tback
    ):
        copy.wait_send()


def per_device(
    patches,
    vis_gain,
    vis_up,
    vis_bias,
    vis_down,
    merge_gain,
    merge_proj,
    text_embed,
    slot_index,
    text_gain,
    text_up,
    text_down,
):
    small = jnp.stack([vis_gain, merge_gain, text_gain])
    slots = jnp.pad(slot_index, (0, 128 - slot_index.shape[0]), constant_values=-1)[None, :]
    any_ = pl.BlockSpec(memory_space=pl.ANY)
    bf16, f32 = jnp.bfloat16, jnp.float32
    vmem = pltpu.VMEM
    return pl.pallas_call(
        step,
        out_shape=jax.ShapeDtypeStruct(text_embed.shape, bf16),
        in_specs=[any_] * 10,
        out_specs=pl.BlockSpec(memory_space=pltpu.VMEM),
        scratch_shapes=[
            vmem((ROWS, D), bf16),
            vmem((3, D), f32),
            vmem((2, 1, QUARTER), f32),
            vmem((2 * ROWS, D), bf16),
            vmem((2 * ROWS, HALF), bf16),
            vmem((HALF, D), bf16),
            vmem((HALF, D), bf16),
            vmem((4 * D, D), bf16),
            vmem((2, NCOL, PART, COLS), bf16),
            vmem((2, NCOL, PART, COLS), bf16),
            vmem((ROWS, D), f32),
            vmem((ROWS, D), bf16),
            vmem((ROWS // 4, 4 * D), bf16),
            vmem((ROWS // 4, D), bf16),
            vmem((BLK, CAP, D), bf16),
            vmem((BLK, CAP, D), bf16),
            vmem((BLK * CAP, D), f32),
            vmem((BLK, 1, 128), jnp.int32),
            vmem((TOK, D), bf16),
            vmem((TOK, D), f32),
            vmem((2, HALF, D), bf16),
            vmem((NCOL, TOK, COLS), bf16),
            vmem((NCOL, TOK, COLS), bf16),
            pltpu.SemaphoreType.DMA((N_SEM,)),
            pltpu.SemaphoreType.DMA((N_SEM,)),
            pltpu.SemaphoreType.DMA((9,)),
        ],
        compiler_params=pltpu.CompilerParams(
            collective_id=0, has_side_effects=True, vmem_limit_bytes=60 * 2**20
        ),
        name="prefill",
    )(
        patches,
        small,
        slots,
        vis_up,
        vis_bias[None, :],
        vis_down,
        merge_proj,
        text_embed,
        text_up,
        text_down,
    )


def solution(mesh):
    placed = (
        P(("seq", "blk"), None),
        P(),
        P("seq", None),
        P("seq"),
        P("seq", None),
        P(),
        P(),
        P(("seq", "blk"), None),
        P(("seq", "blk")),
        P(),
        P("blk", None),
        P("blk", None),
    )
    return jax.shard_map(
        per_device, mesh=mesh, in_specs=placed, out_specs=P(("seq", "blk"), None), check_vma=False
    )
```

```python
import functools

import jax
import jax.numpy as jnp
from jax import lax
from jax.experimental import pallas as pl
from jax.experimental.pallas import tpu as pltpu
from jax.sharding import PartitionSpec as P

MESH = pl.DeviceIdType.MESH
D = 1280
ROWS = 256
TOK = 128
QUARTER = 1280
HALF = 2 * QUARTER
BLK = 32
CAP = 4
COLS = 256
NCOL = D // COLS
PART = 128
SIDES = 3

SHARD = 160

S_VROW, S_UP, S_BIAS, S_DOWN, S_VBACK = 0, 2, 3, 4, 9
S_SLOT, S_A2A, S_TROW, S_TBACK = 14, 15, 16, 19
S_Z, S_O, S_Q, S_PAIR = 34, 35, 39, 43
N_SEM = 51


def normalize(values, row_gain):
    center = values - jnp.mean(values, axis=-1, keepdims=True)
    spread = jnp.mean(center * center, axis=-1, keepdims=True)
    return center * lax.rsqrt(spread + 1e-06) * row_gain


def gelu(v):
    return jax.nn.gelu(v, approximate=True)


def dot(a, b):
    return jnp.dot(a, b, preferred_element_type=jnp.float32)


def dot_t(a, b):
    return lax.dot_general(a, b, (((1,), (1,)), ((), ())), preferred_element_type=jnp.float32)


def before(mask):
    size = mask.shape[1]
    ahead = lax.broadcasted_iota(jnp.int32, (size, size), 0) < lax.broadcasted_iota(
        jnp.int32, (size, size), 1
    )
    ones = jnp.where(mask, 1.0, 0.0).astype(jnp.bfloat16)
    return dot(ones, jnp.where(ahead, 1.0, 0.0).astype(jnp.bfloat16)).astype(jnp.int32)


def step(
    patches,
    vis_gain,
    vis_up,
    bias,
    vis_down,
    merge_gain,
    merge_proj,
    text_embed,
    slots,
    text_gain,
    text_up,
    text_down,
    out,
    rows_v,
    gain_v,
    bias_v,
    x,
    hidden,
    up,
    down,
    proj,
    back_out,
    back_in,
    own,
    normed,
    joined,
    merged,
    send_rows,
    got_rows,
    got_f32,
    all_slots,
    embed_v,
    text_rows,
    xt,
    text_w,
    passing,
    tback_out,
    tback_in,
    send_sem,
    recv_sem,
    local_sem,
):
    seq, blk = lax.axis_index("seq"), lax.axis_index("blk")
    core, half = seq % 2, seq // 2
    px, py, pz = (blk // 2) % 4, blk // 8, (blk % 2) * 2 + half

    def place(cx, cy, cz, cc):
        cx, cy, cz = (cx + 4) % 4, (cy + 4) % 4, (cz + 4) % 4
        return ((cz % 2) * 2 + cc, (cy * 4 + cx) * 2 + cz // 2)

    twin = place(px, py, pz, 1 - core)
    partner = place(px, py, pz + 1 - 2 * core, 1 - core)
    other_hi = place(px, py, pz - 1 + 2 * half, core)
    sides = [
        partner,
        place(px + 1 - 2 * core, py, pz, 1 - core),
        place(px, py + 1 - 2 * core, pz, 1 - core),
    ]
    odd = pz % 2
    users = [place(px + odd + 2 * i, py + odd + 2 * j, pz, core) for i in (0, 1) for j in (0, 1)]

    def remote(src, dst, k, to):
        return pltpu.make_async_remote_copy(
            src_ref=src,
            dst_ref=dst,
            send_sem=send_sem.at[k],
            recv_sem=recv_sem.at[k],
            device_id=to,
            device_id_type=MESH,
        )

    def local(src, dst, k):
        return pltpu.make_async_copy(src, dst, local_sem.at[k])

    gate = pltpu.get_barrier_semaphore()

    def greet(i, carry):
        pl.semaphore_signal(
            gate, inc=1, device_id=(seq, (blk + i) % BLK), device_id_type=MESH
        )
        return carry

    for to in [twin, other_hi] + sides:
        pl.semaphore_signal(gate, inc=1, device_id=to, device_id_type=MESH)
    lax.fori_loop(1, BLK, greet, 0)

    loads = [
        local(patches, rows_v, 0),
        local(vis_gain, gain_v.at[0, 0], 1),
        local(vis_up, up.at[pl.ds(0, QUARTER)], 2),
        local(bias, bias_v.at[0, 0], 3),
        local(vis_down, down.at[pl.ds(0, QUARTER)], 4),
        local(slots, all_slots.at[blk, 0], 5),
        local(text_embed, embed_v, 6),
        local(merge_proj, proj, 7),
        local(merge_gain, gain_v.at[1, 0], 9),
        local(text_gain, gain_v.at[2, 0], 10),
    ]
    for i in (0, 1, 2, 3, 5):
        loads[i].start()
    pl.semaphore_wait(gate, BLK + 4)

    twin_up = remote(vis_up, up.at[pl.ds(QUARTER, QUARTER)], S_UP, twin)
    twin_bias = remote(bias, bias_v.at[1, 0], S_BIAS, twin)
    twin_up.start()
    twin_bias.start()
    for i in (4, 6, 8, 9):
        loads[i].start()
    loads[0].wait()
    loads[1].wait()

    row_copies = []
    for part in range(2):
        rows = pl.ds(part * PART, PART)
        v = rows_v[rows, :].astype(jnp.float32)
        x[pl.ds(ROWS + part * PART, PART), :] = normalize(v, gain_v[0]).astype(jnp.bfloat16)
        copy = remote(x.at[pl.ds(ROWS + part * PART, PART)], x.at[rows], S_VROW + part, partner)
        copy.start()
        row_copies.append(copy)

    def slot(k):
        return text_w.at[core, pl.ds(SHARD * k, SHARD)]

    def o_copy(src, k):
        return remote(src, slot(k), S_O + k, users[k])

    def q_copy(k):
        return remote(passing, slot(4 + k), S_Q + k, users[k])

    z_copy = lambda src: remote(src, passing, S_Z, other_hi)
    for which, source in ((0, text_up), (1, text_down)):

        @pl.when(core == which)
        def _():
            for k in range(1, 4):
                o_copy(source, k).start()

            @pl.when(odd == 0)
            def _():
                local(source, slot(0), 8).start()

            @pl.when(odd == 1)
            def _():
                o_copy(source, 0).start()

    def tell(i, carry):
        remote(slots, all_slots.at[blk, 0], S_SLOT, (seq, (blk + i) % BLK)).start()
        return carry

    lax.fori_loop(1, BLK, tell, 0)

    twin_down = [
        remote(
            vis_down.at[:, pl.ds(j * COLS, COLS)],
            down.at[pl.ds(QUARTER, QUARTER), pl.ds(j * COLS, COLS)],
            S_DOWN + j,
            twin,
        )
        for j in range(NCOL)
    ]
    def up_block(rows, count, quarter):
        def body(j, carry):
            at = pl.multiple_of(j * COLS, COLS)
            h = dot_t(x[rows, :], up[pl.ds(quarter * QUARTER + at, COLS), :])
            h = h + bias_v[quarter, :, pl.ds(at, COLS)]
            hidden[rows, pl.ds(quarter * QUARTER + at, COLS)] = gelu(h).astype(jnp.bfloat16)
            return carry

        lax.fori_loop(0, NCOL, body, 0, unroll=True)

    own_rows, their_rows = pl.ds(ROWS, ROWS), pl.ds(0, ROWS)
    loads[2].wait()
    loads[3].wait()
    up_block(own_rows, ROWS, 0)
    for copy in twin_down:
        copy.start()
    for which, source in ((0, text_up), (1, text_down)):

        @pl.when(core == which)
        def _():
            z_copy(source).start()

    loads[4].wait()
    first, second = pl.ds(0, QUARTER), pl.ds(QUARTER, QUARTER)
    for j in range(NCOL):
        cols = pl.ds(j * COLS, COLS)
        own[:, cols] = dot(hidden[own_rows, first], down[first, cols])
    loads[7].start()
    twin_up.wait_recv()
    twin_bias.wait_recv()
    up_block(own_rows, ROWS, 1)
    for copy in row_copies:
        copy.wait_recv()
    up_block(their_rows, ROWS, 0)
    up_block(their_rows, ROWS, 1)

    z_copy(passing).wait_recv()
    for k in range(1, 4):
        q_copy(k).start()

    @pl.when(odd == 0)
    def _():
        local(passing, slot(4), 11).start()

    @pl.when(odd == 1)
    def _():
        q_copy(0).start()

    back_copies = []
    for j in range(NCOL):
        twin_down[j].wait_recv()
        cols = pl.ds(j * COLS, COLS)
        back_out[j] = dot(hidden[their_rows, :], down[:, cols]).astype(jnp.bfloat16)
        copy = remote(back_out.at[j], back_in.at[j], S_VBACK + j, partner)
        copy.start()
        back_copies.append(copy)
    for j in range(NCOL):
        cols = pl.ds(j * COLS, COLS)
        own[:, cols] = own[:, cols] + dot(hidden[own_rows, second], down[second, cols])

    remote(
        all_slots.at[pl.ds(0, BLK - 1)], all_slots.at[pl.ds(0, BLK - 1)], S_SLOT, twin
    ).wait()
    loads[5].wait()
    slot_rows = all_slots[:, 0, :]
    my_slots = all_slots[blk]
    count = my_slots.shape[1]
    target = (my_slots >> 7) % BLK
    to_target = lax.broadcasted_iota(jnp.int32, (BLK, count), 0) == target
    rank = jnp.sum(jnp.where(to_target, before(to_target), 0), axis=0, keepdims=True)
    goes = target * CAP + rank
    pick = lax.broadcasted_iota(jnp.int32, (BLK * CAP, count), 0) == goes
    pick = jnp.where(pick, 1.0, 0.0).astype(jnp.bfloat16)

    for_me = (slot_rows >> 7) % BLK == blk
    rank_in = before(for_me)
    position = jnp.where(for_me, (slot_rows & (TOK - 1)) + 1, 0)
    lane = lax.broadcasted_iota(jnp.int32, (BLK, BLK * CAP), 1)
    source = lax.broadcasted_iota(jnp.int32, (BLK, BLK * CAP), 0)
    where = jnp.zeros((BLK, BLK * CAP), jnp.int32)
    for r in range(CAP):
        found = jnp.sum(jnp.where(rank_in == r, position, 0), axis=1, keepdims=True)
        where = where + jnp.where(lane == source * CAP + r, found, 0)
    where = jnp.sum(where, axis=0, keepdims=True) - 1
    placing = lax.broadcasted_iota(jnp.int32, (TOK, BLK * CAP), 0) == where
    placing = jnp.where(placing, 1.0, 0.0)

    for j in range(NCOL):
        back_copies[j].wait_recv()
        cols = pl.ds(j * COLS, COLS)
        own[:, cols] = (
            own[:, cols] + back_in[j].astype(jnp.float32) + rows_v[:, cols].astype(jnp.float32)
        )
    loads[8].wait()
    for part in range(2):
        rows = pl.ds(part * PART, PART)
        normed[rows, :] = normalize(own[rows, :], gain_v[1]).astype(jnp.bfloat16)
    to_row = lax.broadcasted_iota(jnp.int32, (ROWS, ROWS), 0)
    from_row = lax.broadcasted_iota(jnp.int32, (ROWS, ROWS), 1)
    order = from_row == 4 * (to_row & 63) + (to_row >> 6)
    order = jnp.where(order, 1.0, 0.0).astype(jnp.bfloat16)
    for j in range(NCOL):
        moved = dot(order, normed[:, pl.ds(j * COLS, COLS)]).astype(jnp.bfloat16)
        for k in range(4):
            joined[:, pl.ds(k * D + j * COLS, COLS)] = moved[k * 64 : (k + 1) * 64, :]
    loads[7].wait()
    for j in range(NCOL):
        cols = pl.ds(j * COLS, COLS)
        merged[:, cols] = dot(joined[...], proj[:, cols]).astype(jnp.bfloat16)
    spread_rows = dot(pick, merged[...])
    for t in range(BLK):
        send_rows[t] = spread_rows[t * CAP : (t + 1) * CAP, :].astype(jnp.bfloat16)

    def send(i, carry):
        to = (blk + i) % BLK
        remote(send_rows.at[to], got_rows.at[blk], S_A2A, (seq, to)).start()
        return carry

    lax.fori_loop(1, BLK, send, 0)
    got_rows[blk] = send_rows[blk]

    for k in range(1, 4):
        o_copy(passing, k).wait_recv()
        q_copy(k).wait_recv()

    @pl.when(odd == 0)
    def _():
        local(passing, slot(0), 8).wait()
        local(passing, slot(4), 11).wait()

    @pl.when(odd == 1)
    def _():
        o_copy(passing, 0).wait_recv()
        q_copy(0).wait_recv()

    pair_copies = [remote(slot(k), slot(k), S_PAIR + k, twin) for k in range(8)]
    for copy in pair_copies:
        copy.start()

    remote(
        send_rows.at[pl.ds(0, BLK - 1)], got_rows.at[pl.ds(0, BLK - 1)], S_A2A, twin
    ).wait()
    for t in range(BLK):
        got_f32[pl.ds(t * CAP, CAP), :] = got_rows[t].astype(jnp.float32)
    loads[6].wait()
    placed = dot(placing.astype(jnp.bfloat16), got_f32[...].astype(jnp.bfloat16))
    filled = jnp.sum(placing, axis=1, keepdims=True) > 0.5
    text_rows[...] = jnp.where(filled, placed, embed_v[...].astype(jnp.float32))

    own_tok = pl.ds(SIDES * TOK, TOK)
    loads[9].wait()
    xt[own_tok, :] = normalize(text_rows[...], gain_v[2]).astype(jnp.bfloat16)
    text_row = [
        remote(xt.at[own_tok], xt.at[pl.ds(i * TOK, TOK)], S_TROW + i, to)
        for i, to in enumerate(sides)
    ]
    for copy in text_row:
        copy.start()
    for copy in pair_copies:
        copy.wait_recv()

    def text_up_block(rows):
        def body(j, carry):
            at = pl.multiple_of(j * COLS, COLS)
            h = dot_t(xt[rows, :], text_w[0, pl.ds(at, COLS), :])
            hidden[rows, pl.ds(at, COLS)] = gelu(h).astype(jnp.bfloat16)
            return carry

        lax.fori_loop(0, NCOL, body, 0, unroll=True)

    text_up_block(own_tok)
    for j in range(NCOL):
        cols = pl.ds(j * COLS, COLS)
        text_rows[:, cols] = text_rows[:, cols] + dot(hidden[own_tok, first], text_w[1, :, cols])
    for copy in text_row:
        copy.wait_recv()
    theirs = pl.ds(0, SIDES * TOK)
    text_up_block(theirs)
    tback = []
    for j in range(NCOL):
        cols = pl.ds(j * COLS, COLS)
        part = dot(hidden[theirs, first], text_w[1, :, cols]).astype(jnp.bfloat16)
        for i, to in enumerate(sides):
            tback_out[i, j] = part[i * TOK : (i + 1) * TOK, :]
            copy = remote(tback_out.at[i, j], tback_in.at[i, j], S_TBACK + i * NCOL + j, to)
            copy.start()
            tback.append(copy)
    for j in range(NCOL):
        cols = pl.ds(j * COLS, COLS)
        total = text_rows[:, cols]
        for i in range(SIDES):
            tback[j * SIDES + i].wait_recv()
            total = total + tback_in[i, j].astype(jnp.float32)
        out[:, cols] = total.astype(jnp.bfloat16)

    z_copy(passing).wait_send()
    for k in range(1, 4):
        o_copy(passing, k).wait_send()
        q_copy(k).wait_send()

    @pl.when(odd == 1)
    def _():
        o_copy(passing, 0).wait_send()
        q_copy(0).wait_send()

    for copy in (
        row_copies
        + [twin_up, twin_bias]
        + twin_down
        + back_copies
        + pair_copies
        + text_row
        + tback
    ):
        copy.wait_send()


def per_device(
    patches,
    vis_gain,
    vis_up,
    vis_bias,
    vis_down,
    merge_gain,
    merge_proj,
    text_embed,
    slot_index,
    text_gain,
    text_up,
    text_down,
):
    any_ = pl.BlockSpec(memory_space=pl.ANY)
    bf16, f32 = jnp.bfloat16, jnp.float32
    vmem = pltpu.VMEM
    return pl.pallas_call(
        step,
        out_shape=jax.ShapeDtypeStruct(text_embed.shape, bf16),
        in_specs=[any_] * 12,
        out_specs=pl.BlockSpec(memory_space=pltpu.VMEM),
        scratch_shapes=[
            vmem((ROWS, D), bf16),
            vmem((3, 1, D), f32),
            vmem((2, 1, QUARTER), f32),
            vmem((2 * ROWS, D), bf16),
            vmem((2 * ROWS, HALF), bf16),
            vmem((HALF, D), bf16),
            vmem((HALF, D), bf16),
            vmem((4 * D, D), bf16),
            vmem((NCOL, ROWS, COLS), bf16),
            vmem((NCOL, ROWS, COLS), bf16),
            vmem((ROWS, D), f32),
            vmem((ROWS, D), bf16),
            vmem((ROWS // 4, 4 * D), bf16),
            vmem((ROWS // 4, D), bf16),
            vmem((BLK, CAP, D), bf16),
            vmem((BLK, CAP, D), bf16),
            vmem((BLK * CAP, D), f32),
            vmem((BLK, 1, slot_index.shape[0]), jnp.int32),
            vmem((TOK, D), bf16),
            vmem((TOK, D), f32),
            vmem(((SIDES + 1) * TOK, D), bf16),
            vmem((2, QUARTER, D), bf16),
            vmem((SHARD, D), bf16),
            vmem((SIDES, NCOL, TOK, COLS), bf16),
            vmem((SIDES, NCOL, TOK, COLS), bf16),
            pltpu.SemaphoreType.DMA((N_SEM,)),
            pltpu.SemaphoreType.DMA((N_SEM,)),
            pltpu.SemaphoreType.DMA((12,)),
        ],
        compiler_params=pltpu.CompilerParams(
            collective_id=0, has_side_effects=True, vmem_limit_bytes=60 * 2**20
        ),
        name="prefill",
    )(
        patches,
        vis_gain,
        vis_up,
        vis_bias,
        vis_down,
        merge_gain,
        merge_proj,
        text_embed,
        slot_index,
        text_gain,
        text_up,
        text_down,
    )


def solution(mesh):
    placed = (
        P(("seq", "blk"), None),
        P(),
        P("seq", None),
        P("seq"),
        P("seq", None),
        P(),
        P(),
        P(("seq", "blk"), None),
        P(("seq", "blk")),
        P(),
        P("blk", None),
        P("blk", None),
    )
    return jax.shard_map(
        per_device, mesh=mesh, in_specs=placed, out_specs=P(("seq", "blk"), None), check_vma=False
    )
```

```python
import functools

import jax
import jax.numpy as jnp
from jax import lax
from jax.experimental import pallas as pl
from jax.experimental.pallas import tpu as pltpu
from jax.sharding import PartitionSpec as P

MESH = pl.DeviceIdType.MESH
D = 1280
ROWS = 256
TOK = 128
QUARTER = 1280
HALF = 2 * QUARTER
BLK = 32
CAP = 4
COLS = 256
NCOL = D // COLS
PART = 64
NROW = ROWS // PART
SIDES = 3

SHARD = 160

S_VROW, S_UP, S_BIAS, S_DOWN, S_VBACK = 0, 4, 5, 6, 11
S_SLOT, S_A2A, S_TROW, S_TBACK = 16, 17, 18, 21
S_Z, S_O, S_Q, S_PAIR = 36, 38, 42, 50
N_SEM = 62


def normalize(values, row_gain):
    center = values - jnp.mean(values, axis=-1, keepdims=True)
    spread = jnp.mean(center * center, axis=-1, keepdims=True)
    return center * lax.rsqrt(spread + 1e-06) * row_gain


def gelu(v):
    return jax.nn.gelu(v, approximate=True)


def dot(a, b):
    return jnp.dot(a, b, preferred_element_type=jnp.float32)


def dot_t(a, b):
    return lax.dot_general(a, b, (((1,), (1,)), ((), ())), preferred_element_type=jnp.float32)


def before(mask):
    size = mask.shape[1]
    ahead = lax.broadcasted_iota(jnp.int32, (size, size), 0) < lax.broadcasted_iota(
        jnp.int32, (size, size), 1
    )
    ones = jnp.where(mask, 1.0, 0.0).astype(jnp.bfloat16)
    return dot(ones, jnp.where(ahead, 1.0, 0.0).astype(jnp.bfloat16)).astype(jnp.int32)


def step(
    patches,
    vis_gain,
    vis_up,
    bias,
    vis_down,
    merge_gain,
    merge_proj,
    text_embed,
    slots,
    text_gain,
    text_up,
    text_down,
    out,
    rows_v,
    gain_v,
    bias_v,
    x,
    hidden,
    up,
    down,
    proj,
    back_out,
    back_in,
    own,
    normed,
    joined,
    merged,
    send_rows,
    got_rows,
    got_f32,
    all_slots,
    embed_v,
    text_rows,
    xt,
    text_w,
    passing,
    tback_out,
    tback_in,
    send_sem,
    recv_sem,
    local_sem,
    line_sem,
    plane_sem,
    twin_sem,
):
    seq, blk = lax.axis_index("seq"), lax.axis_index("blk")
    core, half = seq % 2, seq // 2
    px, py, pz = (blk // 2) % 4, blk // 8, (blk % 2) * 2 + half

    def place(cx, cy, cz, cc):
        cx, cy, cz = (cx + 4) % 4, (cy + 4) % 4, (cz + 4) % 4
        return ((cz % 2) * 2 + cc, (cy * 4 + cx) * 2 + cz // 2)

    twin = place(px, py, pz, 1 - core)
    partner = place(px, py, pz + 1 - 2 * core, 1 - core)
    other_hi = place(px, py, pz - 1 + 2 * half, core)
    sides = [
        partner,
        place(px + 1 - 2 * core, py, pz, 1 - core),
        place(px, py + 1 - 2 * core, pz, 1 - core),
    ]
    odd = pz % 2
    users = [place(px + odd + 2 * i, py + odd + 2 * j, pz, core) for i in (0, 1) for j in (0, 1)]

    def remote(src, dst, k, to):
        return pltpu.make_async_remote_copy(
            src_ref=src,
            dst_ref=dst,
            send_sem=send_sem.at[k],
            recv_sem=recv_sem.at[k],
            device_id=to,
            device_id_type=MESH,
        )

    def local(src, dst, k):
        return pltpu.make_async_copy(src, dst, local_sem.at[k])

    gate = pltpu.get_barrier_semaphore()
    line_x = [place(px + d, py, pz, core) for d in (1, 2, 3)]
    line_y = [place(px, py + d, pz, core) for d in (1, 2, 3)]
    across = place(px, py, pz + 2, core)
    near = [partner, twin, other_hi, across] + line_x + line_y
    for to in near:
        pl.semaphore_signal(gate, inc=1, device_id=to, device_id_type=MESH)

    loads = [
        local(patches, rows_v, 0),
        local(vis_gain, gain_v.at[0, 0], 1),
        local(vis_up, up.at[pl.ds(0, QUARTER)], 2),
        local(bias, bias_v.at[0, 0], 3),
        local(vis_down, down.at[pl.ds(0, QUARTER)], 4),
        local(slots, all_slots.at[blk, 0], 5),
        local(text_embed, embed_v, 6),
        local(merge_proj, proj, 7),
        local(merge_gain, gain_v.at[1, 0], 9),
        local(text_gain, gain_v.at[2, 0], 10),
    ]
    for i in (0, 1, 2, 3, 5):
        loads[i].start()
    pl.semaphore_wait(gate, len(near))

    def z_copy(src, h):
        part = pl.ds(h * SHARD // 2, SHARD // 2)
        return remote(src.at[part], passing.at[part], S_Z + h, other_hi)

    def z_start(h):
        for which, source in ((0, text_up), (1, text_down)):

            @pl.when(core == which)
            def _():
                z_copy(source, h).start()

    twin_up = remote(vis_up, up.at[pl.ds(QUARTER, QUARTER)], S_UP, twin)
    twin_bias = remote(bias, bias_v.at[1, 0], S_BIAS, twin)
    twin_up.start()
    twin_bias.start()
    for to in line_y:
        pl.semaphore_signal(line_sem, inc=1, device_id=to, device_id_type=MESH)
    pl.semaphore_signal(twin_sem, inc=1, device_id=twin, device_id_type=MESH)
    for i in (4, 6, 8, 9):
        loads[i].start()
    loads[0].wait()
    loads[1].wait()

    row_copies = []
    for part in range(NROW):
        rows = pl.ds(part * PART, PART)
        v = rows_v[rows, :].astype(jnp.float32)
        x[pl.ds(ROWS + part * PART, PART), :] = normalize(v, gain_v[0]).astype(jnp.bfloat16)
        copy = remote(x.at[pl.ds(ROWS + part * PART, PART)], x.at[rows], S_VROW + part, partner)
        copy.start()
        row_copies.append(copy)
    pl.semaphore_wait(line_sem, len(line_y))
    pl.semaphore_signal(plane_sem, inc=1, device_id=across, device_id_type=MESH)

    def slot(k):
        return text_w.at[core, pl.ds(SHARD * k, SHARD)]

    def o_copy(src, k):
        return remote(src, slot(k), S_O + k, users[k])

    def half_slot(k, h):
        return text_w.at[core, pl.ds(SHARD * k + SHARD // 2 * h, SHARD // 2)]

    def q_copy(k, h):
        part = passing.at[pl.ds(h * SHARD // 2, SHARD // 2)]
        return remote(part, half_slot(4 + k, h), S_Q + 2 * k + h, users[k])

    def q_local(h):
        part = passing.at[pl.ds(h * SHARD // 2, SHARD // 2)]
        return local(part, half_slot(4, h), 11 + h)

    def pass_on(h):
        z_copy(passing, h).wait_recv()
        for k in range(1, 4):
            q_copy(k, h).start()

        @pl.when(odd == 0)
        def _():
            q_local(h).start()

        @pl.when(odd == 1)
        def _():
            q_copy(0, h).start()

    def passed_on(h):
        for k in range(1, 4):
            q_copy(k, h).wait_recv()

        @pl.when(odd == 0)
        def _():
            q_local(h).wait()

        @pl.when(odd == 1)
        def _():
            q_copy(0, h).wait_recv()

    for which, source in ((0, text_up), (1, text_down)):

        @pl.when(core == which)
        def _():
            for k in range(1, 4):
                o_copy(source, k).start()

            @pl.when(odd == 0)
            def _():
                local(source, slot(0), 8).start()

            @pl.when(odd == 1)
            def _():
                o_copy(source, 0).start()

    pl.semaphore_wait(plane_sem, 1)
    pl.semaphore_wait(twin_sem, 1)
    def tell(i, carry):
        remote(slots, all_slots.at[blk, 0], S_SLOT, (seq, (blk + i) % BLK)).start()
        return carry

    lax.fori_loop(1, BLK, tell, 0)

    twin_down = [
        remote(
            vis_down.at[:, pl.ds(j * COLS, COLS)],
            down.at[pl.ds(QUARTER, QUARTER), pl.ds(j * COLS, COLS)],
            S_DOWN + j,
            twin,
        )
        for j in range(NCOL)
    ]
    def up_block(rows, count, quarter):
        def body(j, carry):
            at = pl.multiple_of(j * COLS, COLS)
            h = dot_t(x[rows, :], up[pl.ds(quarter * QUARTER + at, COLS), :])
            h = h + bias_v[quarter, :, pl.ds(at, COLS)]
            hidden[rows, pl.ds(quarter * QUARTER + at, COLS)] = gelu(h).astype(jnp.bfloat16)
            return carry

        lax.fori_loop(0, NCOL, body, 0, unroll=True)

    own_rows, their_rows = pl.ds(ROWS, ROWS), pl.ds(0, ROWS)
    loads[2].wait()
    loads[3].wait()
    up_block(own_rows, ROWS, 0)
    for copy in twin_down:
        copy.start()
    loads[4].wait()
    first, second = pl.ds(0, QUARTER), pl.ds(QUARTER, QUARTER)
    for j in range(NCOL):
        cols = pl.ds(j * COLS, COLS)
        own[:, cols] = dot(hidden[own_rows, first], down[first, cols])
    loads[7].start()
    twin_up.wait_recv()
    twin_bias.wait_recv()
    up_block(own_rows, ROWS, 1)
    for copy in row_copies:
        copy.wait_send()
    z_start(0)
    for copy in row_copies:
        copy.wait_recv()
    up_block(their_rows, ROWS, 0)
    up_block(their_rows, ROWS, 1)

    back_copies = []
    for j in range(NCOL):
        twin_down[j].wait_recv()
        cols = pl.ds(j * COLS, COLS)
        back_out[j] = dot(hidden[their_rows, :], down[:, cols]).astype(jnp.bfloat16)
        copy = remote(back_out.at[j], back_in.at[j], S_VBACK + j, partner)
        copy.start()
        back_copies.append(copy)
    pass_on(0)
    for j in range(NCOL):
        cols = pl.ds(j * COLS, COLS)
        own[:, cols] = own[:, cols] + dot(hidden[own_rows, second], down[second, cols])

    remote(
        all_slots.at[pl.ds(0, BLK - 1)], all_slots.at[pl.ds(0, BLK - 1)], S_SLOT, twin
    ).wait()
    loads[5].wait()
    slot_rows = all_slots[:, 0, :]
    my_slots = all_slots[blk]
    count = my_slots.shape[1]
    target = (my_slots >> 7) % BLK
    to_target = lax.broadcasted_iota(jnp.int32, (BLK, count), 0) == target
    rank = jnp.sum(jnp.where(to_target, before(to_target), 0), axis=0, keepdims=True)
    goes = target * CAP + rank
    pick = lax.broadcasted_iota(jnp.int32, (BLK * CAP, count), 0) == goes
    pick = jnp.where(pick, 1.0, 0.0).astype(jnp.bfloat16)

    for_me = (slot_rows >> 7) % BLK == blk
    rank_in = before(for_me)
    position = jnp.where(for_me, (slot_rows & (TOK - 1)) + 1, 0)
    lane = lax.broadcasted_iota(jnp.int32, (BLK, BLK * CAP), 1)
    source = lax.broadcasted_iota(jnp.int32, (BLK, BLK * CAP), 0)
    where = jnp.zeros((BLK, BLK * CAP), jnp.int32)
    for r in range(CAP):
        found = jnp.sum(jnp.where(rank_in == r, position, 0), axis=1, keepdims=True)
        where = where + jnp.where(lane == source * CAP + r, found, 0)
    where = jnp.sum(where, axis=0, keepdims=True) - 1
    placing = lax.broadcasted_iota(jnp.int32, (TOK, BLK * CAP), 0) == where
    placing = jnp.where(placing, 1.0, 0.0)

    for k in range(1, 4):
        o_copy(passing, k).wait_recv()

    @pl.when(odd == 0)
    def _():
        local(passing, slot(0), 8).wait()

    @pl.when(odd == 1)
    def _():
        o_copy(passing, 0).wait_recv()

    pair_o = [remote(slot(k), slot(k), S_PAIR + k, twin) for k in range(4)]
    for copy in pair_o:
        copy.start()

    for j in range(NCOL):
        back_copies[j].wait_recv()
        cols = pl.ds(j * COLS, COLS)
        own[:, cols] = (
            own[:, cols] + back_in[j].astype(jnp.float32) + rows_v[:, cols].astype(jnp.float32)
        )
    z_start(1)
    loads[8].wait()
    for part in range(NROW):
        rows = pl.ds(part * PART, PART)
        normed[rows, :] = normalize(own[rows, :], gain_v[1]).astype(jnp.bfloat16)
    to_row = lax.broadcasted_iota(jnp.int32, (ROWS, ROWS), 0)
    from_row = lax.broadcasted_iota(jnp.int32, (ROWS, ROWS), 1)
    order = from_row == 4 * (to_row & 63) + (to_row >> 6)
    order = jnp.where(order, 1.0, 0.0).astype(jnp.bfloat16)
    for j in range(NCOL):
        moved = dot(order, normed[:, pl.ds(j * COLS, COLS)]).astype(jnp.bfloat16)
        for k in range(4):
            joined[:, pl.ds(k * D + j * COLS, COLS)] = moved[k * 64 : (k + 1) * 64, :]
    loads[7].wait()
    for j in range(NCOL):
        cols = pl.ds(j * COLS, COLS)
        merged[:, cols] = dot(joined[...], proj[:, cols]).astype(jnp.bfloat16)
    spread_rows = dot(pick, merged[...])
    for t in range(BLK):
        send_rows[t] = spread_rows[t * CAP : (t + 1) * CAP, :].astype(jnp.bfloat16)

    def send(i, carry):
        to = (blk + i) % BLK
        remote(send_rows.at[to], got_rows.at[blk], S_A2A, (seq, to)).start()
        return carry

    lax.fori_loop(1, BLK, send, 0)
    got_rows[blk] = send_rows[blk]
    pass_on(1)

    remote(
        send_rows.at[pl.ds(0, BLK - 1)], got_rows.at[pl.ds(0, BLK - 1)], S_A2A, twin
    ).wait()
    for t in range(BLK):
        got_f32[pl.ds(t * CAP, CAP), :] = got_rows[t].astype(jnp.float32)
    loads[6].wait()
    placed = dot(placing.astype(jnp.bfloat16), got_f32[...].astype(jnp.bfloat16))
    filled = jnp.sum(placing, axis=1, keepdims=True) > 0.5
    text_rows[...] = jnp.where(filled, placed, embed_v[...].astype(jnp.float32))

    own_tok = pl.ds(SIDES * TOK, TOK)
    loads[9].wait()
    xt[own_tok, :] = normalize(text_rows[...], gain_v[2]).astype(jnp.bfloat16)
    text_row = [
        remote(xt.at[own_tok], xt.at[pl.ds(i * TOK, TOK)], S_TROW + i, to)
        for i, to in enumerate(sides)
    ]
    for copy in text_row:
        copy.start()

    def text_up_block(part):
        for start, size in ((0, 256), (256, 256), (512, 128)):
            at = pl.ds(part * 4 * SHARD + start, size)
            hidden[:, at] = gelu(dot_t(xt[...], text_w[0, at, :])).astype(jnp.bfloat16)

    theirs = pl.ds(0, SIDES * TOK)
    pair_q = []
    for h in range(2):
        passed_on(h)
        for k in range(4):
            part = half_slot(4 + k, h)
            copy = remote(part, part, S_PAIR + 4 + 4 * h + k, twin)
            copy.start()
            pair_q.append(copy)
    for copy in pair_o:
        copy.wait_recv()
    for copy in text_row:
        copy.wait_recv()
    text_up_block(0)
    for copy in pair_q:
        copy.wait_recv()
    text_up_block(1)
    tback = []
    for j in range(NCOL):
        cols = pl.ds(j * COLS, COLS)
        part = dot(hidden[theirs, first], text_w[1, :, cols]).astype(jnp.bfloat16)
        for i, to in enumerate(sides):
            tback_out[i, j] = part[i * TOK : (i + 1) * TOK, :]
            copy = remote(tback_out.at[i, j], tback_in.at[i, j], S_TBACK + i * NCOL + j, to)
            copy.start()
            tback.append(copy)
    for j in range(NCOL):
        cols = pl.ds(j * COLS, COLS)
        text_rows[:, cols] = text_rows[:, cols] + dot(hidden[own_tok, first], text_w[1, :, cols])
    for j in range(NCOL):
        cols = pl.ds(j * COLS, COLS)
        total = text_rows[:, cols]
        for i in range(SIDES):
            tback[j * SIDES + i].wait_recv()
            total = total + tback_in[i, j].astype(jnp.float32)
        out[:, cols] = total.astype(jnp.bfloat16)

    for h in range(2):
        z_copy(passing, h).wait_send()
    for k in range(1, 4):
        o_copy(passing, k).wait_send()
        for h in range(2):
            q_copy(k, h).wait_send()

    @pl.when(odd == 1)
    def _():
        o_copy(passing, 0).wait_send()
        for h in range(2):
            q_copy(0, h).wait_send()

    for copy in (
        [twin_up, twin_bias]
        + twin_down
        + back_copies
        + pair_o
        + pair_q
        + text_row
        + tback
    ):
        copy.wait_send()


def per_device(
    patches,
    vis_gain,
    vis_up,
    vis_bias,
    vis_down,
    merge_gain,
    merge_proj,
    text_embed,
    slot_index,
    text_gain,
    text_up,
    text_down,
):
    any_ = pl.BlockSpec(memory_space=pl.ANY)
    bf16, f32 = jnp.bfloat16, jnp.float32
    vmem = pltpu.VMEM
    return pl.pallas_call(
        step,
        out_shape=jax.ShapeDtypeStruct(text_embed.shape, bf16),
        in_specs=[any_] * 12,
        out_specs=pl.BlockSpec(memory_space=pltpu.VMEM),
        scratch_shapes=[
            vmem((ROWS, D), bf16),
            vmem((3, 1, D), f32),
            vmem((2, 1, QUARTER), f32),
            vmem((2 * ROWS, D), bf16),
            vmem((2 * ROWS, HALF), bf16),
            vmem((HALF, D), bf16),
            vmem((HALF, D), bf16),
            vmem((4 * D, D), bf16),
            vmem((NCOL, ROWS, COLS), bf16),
            vmem((NCOL, ROWS, COLS), bf16),
            vmem((ROWS, D), f32),
            vmem((ROWS, D), bf16),
            vmem((ROWS // 4, 4 * D), bf16),
            vmem((ROWS // 4, D), bf16),
            vmem((BLK, CAP, D), bf16),
            vmem((BLK, CAP, D), bf16),
            vmem((BLK * CAP, D), f32),
            vmem((BLK, 1, slot_index.shape[0]), jnp.int32),
            vmem((TOK, D), bf16),
            vmem((TOK, D), f32),
            vmem(((SIDES + 1) * TOK, D), bf16),
            vmem((2, QUARTER, D), bf16),
            vmem((SHARD, D), bf16),
            vmem((SIDES, NCOL, TOK, COLS), bf16),
            vmem((SIDES, NCOL, TOK, COLS), bf16),
            pltpu.SemaphoreType.DMA((N_SEM,)),
            pltpu.SemaphoreType.DMA((N_SEM,)),
            pltpu.SemaphoreType.DMA((13,)),
            pltpu.SemaphoreType.REGULAR,
            pltpu.SemaphoreType.REGULAR,
            pltpu.SemaphoreType.REGULAR,
        ],
        compiler_params=pltpu.CompilerParams(
            collective_id=0, has_side_effects=True, vmem_limit_bytes=60 * 2**20
        ),
        name="prefill",
    )(
        patches,
        vis_gain,
        vis_up,
        vis_bias,
        vis_down,
        merge_gain,
        merge_proj,
        text_embed,
        slot_index,
        text_gain,
        text_up,
        text_down,
    )


def solution(mesh):
    placed = (
        P(("seq", "blk"), None),
        P(),
        P("seq", None),
        P("seq"),
        P("seq", None),
        P(),
        P(),
        P(("seq", "blk"), None),
        P(("seq", "blk")),
        P(),
        P("blk", None),
        P("blk", None),
    )
    return jax.shard_map(
        per_device, mesh=mesh, in_specs=placed, out_specs=P(("seq", "blk"), None), check_vma=False
    )
```

```python
import functools

import jax
import jax.numpy as jnp
from jax import lax
from jax.experimental import pallas as pl
from jax.experimental.pallas import tpu as pltpu
from jax.sharding import PartitionSpec as P

MESH = pl.DeviceIdType.MESH
D = 1280
ROWS = 256
TOK = 128
QUARTER = 1280
HALF = 2 * QUARTER
BLK = 32
CAP = 4
COLS = 256
NCOL = D // COLS
PART = 64
NROW = ROWS // PART
SIDES = 3

SHARD = 160

S_VROW, S_UP, S_BIAS, S_DOWN, S_VBACK = 0, 4, 5, 6, 11
S_SLOT, S_A2A, S_TROW, S_TBACK = 16, 17, 18, 21
S_Z, S_O, S_Q, S_PAIR = 36, 38, 42, 50
N_SEM = 62


def normalize(values, row_gain):
    center = values - jnp.mean(values, axis=-1, keepdims=True)
    spread = jnp.mean(center * center, axis=-1, keepdims=True)
    return center * lax.rsqrt(spread + 1e-06) * row_gain


def gelu(v):
    return jax.nn.gelu(v, approximate=True)


def dot(a, b):
    return jnp.dot(a, b, preferred_element_type=jnp.float32)


def dot_t(a, b):
    return lax.dot_general(a, b, (((1,), (1,)), ((), ())), preferred_element_type=jnp.float32)


def before(mask):
    size = mask.shape[1]
    ahead = lax.broadcasted_iota(jnp.int32, (size, size), 0) < lax.broadcasted_iota(
        jnp.int32, (size, size), 1
    )
    ones = jnp.where(mask, 1.0, 0.0).astype(jnp.bfloat16)
    return dot(ones, jnp.where(ahead, 1.0, 0.0).astype(jnp.bfloat16)).astype(jnp.int32)


def step(
    patches,
    vis_gain,
    vis_up,
    bias,
    vis_down,
    merge_gain,
    merge_proj,
    text_embed,
    slots,
    text_gain,
    text_up,
    text_down,
    out,
    rows_v,
    gain_v,
    bias_v,
    x,
    hidden,
    up,
    down,
    proj,
    back_out,
    back_in,
    own,
    normed,
    joined,
    merged,
    send_rows,
    got_rows,
    got_f32,
    all_slots,
    embed_v,
    text_rows,
    xt,
    text_w,
    passing,
    tback_out,
    tback_in,
    send_sem,
    recv_sem,
    local_sem,
    line_sem,
    plane_sem,
    twin_sem,
):
    seq, blk = lax.axis_index("seq"), lax.axis_index("blk")
    core, half = seq % 2, seq // 2
    px, py, pz = (blk // 2) % 4, blk // 8, (blk % 2) * 2 + half

    def place(cx, cy, cz, cc):
        cx, cy, cz = (cx + 4) % 4, (cy + 4) % 4, (cz + 4) % 4
        return ((cz % 2) * 2 + cc, (cy * 4 + cx) * 2 + cz // 2)

    twin = place(px, py, pz, 1 - core)
    partner = place(px, py, pz + 1 - 2 * core, 1 - core)
    other_hi = place(px, py, pz - 1 + 2 * half, core)
    sides = [
        partner,
        place(px + 1 - 2 * core, py, pz, 1 - core),
        place(px, py + 1 - 2 * core, pz, 1 - core),
    ]
    odd = pz % 2
    users = [place(px + odd + 2 * i, py + odd + 2 * j, pz, core) for i in (0, 1) for j in (0, 1)]

    def remote(src, dst, k, to):
        return pltpu.make_async_remote_copy(
            src_ref=src,
            dst_ref=dst,
            send_sem=send_sem.at[k],
            recv_sem=recv_sem.at[k],
            device_id=to,
            device_id_type=MESH,
        )

    def local(src, dst, k):
        return pltpu.make_async_copy(src, dst, local_sem.at[k])

    gate = pltpu.get_barrier_semaphore()
    line_x = [place(px + d, py, pz, core) for d in (1, 2, 3)]
    line_y = [place(px, py + d, pz, core) for d in (1, 2, 3)]
    across = place(px, py, pz + 2, core)
    near = [partner, twin, other_hi, across] + line_x + line_y
    for to in near:
        pl.semaphore_signal(gate, inc=1, device_id=to, device_id_type=MESH)

    loads = [
        local(patches, rows_v, 0),
        local(vis_gain, gain_v.at[0, 0], 1),
        local(vis_up, up.at[pl.ds(0, QUARTER)], 2),
        local(bias, bias_v.at[0, 0], 3),
        local(vis_down, down.at[pl.ds(0, QUARTER)], 4),
        local(slots, all_slots.at[blk, 0], 5),
        local(text_embed, embed_v, 6),
        local(merge_proj, proj, 7),
        local(merge_gain, gain_v.at[1, 0], 9),
        local(text_gain, gain_v.at[2, 0], 10),
    ]
    for i in (0, 1, 2, 3, 5):
        loads[i].start()
    pl.semaphore_wait(gate, len(near))

    def z_copy(src, h):
        part = pl.ds(h * SHARD // 2, SHARD // 2)
        return remote(src.at[part], passing.at[part], S_Z + h, other_hi)

    def z_start(h):
        for which, source in ((0, text_up), (1, text_down)):

            @pl.when(core == which)
            def _():
                z_copy(source, h).start()

    twin_up = remote(vis_up, up.at[pl.ds(QUARTER, QUARTER)], S_UP, twin)
    twin_bias = remote(bias, bias_v.at[1, 0], S_BIAS, twin)
    twin_up.start()
    twin_bias.start()
    for to in line_y:
        pl.semaphore_signal(line_sem, inc=1, device_id=to, device_id_type=MESH)
    pl.semaphore_signal(twin_sem, inc=1, device_id=twin, device_id_type=MESH)
    for i in (4, 6, 8, 9):
        loads[i].start()
    loads[0].wait()
    loads[1].wait()

    row_copies = []
    for part in range(NROW):
        rows = pl.ds(part * PART, PART)
        v = rows_v[rows, :].astype(jnp.float32)
        x[pl.ds(ROWS + part * PART, PART), :] = normalize(v, gain_v[0]).astype(jnp.bfloat16)
        copy = remote(x.at[pl.ds(ROWS + part * PART, PART)], x.at[rows], S_VROW + part, partner)
        copy.start()
        row_copies.append(copy)
    pl.semaphore_wait(line_sem, len(line_y))
    pl.semaphore_signal(plane_sem, inc=1, device_id=across, device_id_type=MESH)

    def slot(k):
        return text_w.at[core, pl.ds(SHARD * k, SHARD)]

    def o_copy(src, k):
        return remote(src, slot(k), S_O + k, users[k])

    def half_slot(k, h):
        return text_w.at[core, pl.ds(SHARD * k + SHARD // 2 * h, SHARD // 2)]

    def q_copy(k, h):
        part = passing.at[pl.ds(h * SHARD // 2, SHARD // 2)]
        return remote(part, half_slot(4 + k, h), S_Q + 2 * k + h, users[k])

    def q_local(h):
        part = passing.at[pl.ds(h * SHARD // 2, SHARD // 2)]
        return local(part, half_slot(4, h), 11 + h)

    def pass_on(h):
        z_copy(passing, h).wait_recv()
        for which, order in ((0, (1, 2, 3)), (1, (2, 1, 3))):

            @pl.when(core == which)
            def _():
                for k in order:
                    q_copy(k, h).start()

        @pl.when(odd == 0)
        def _():
            q_local(h).start()

        @pl.when(odd == 1)
        def _():
            q_copy(0, h).start()

    def passed_on(h):
        for k in range(1, 4):
            q_copy(k, h).wait_recv()

        @pl.when(odd == 0)
        def _():
            q_local(h).wait()

        @pl.when(odd == 1)
        def _():
            q_copy(0, h).wait_recv()

    for which, source in ((0, text_up), (1, text_down)):

        @pl.when(core == which)
        def _():
            for k in (1, 2, 3) if which == 0 else (2, 1, 3):
                o_copy(source, k).start()

            @pl.when(odd == 0)
            def _():
                local(source, slot(0), 8).start()

            @pl.when(odd == 1)
            def _():
                o_copy(source, 0).start()

    pl.semaphore_wait(plane_sem, 1)
    pl.semaphore_wait(twin_sem, 1)
    def tell(i, carry):
        remote(slots, all_slots.at[blk, 0], S_SLOT, (seq, (blk + i) % BLK)).start()
        return carry

    lax.fori_loop(1, BLK, tell, 0)

    twin_down = [
        remote(
            vis_down.at[:, pl.ds(j * COLS, COLS)],
            down.at[pl.ds(QUARTER, QUARTER), pl.ds(j * COLS, COLS)],
            S_DOWN + j,
            twin,
        )
        for j in range(NCOL)
    ]
    def up_block(rows, count, quarter):
        def body(j, carry):
            at = pl.multiple_of(j * COLS, COLS)
            h = dot_t(x[rows, :], up[pl.ds(quarter * QUARTER + at, COLS), :])
            h = h + bias_v[quarter, :, pl.ds(at, COLS)]
            hidden[rows, pl.ds(quarter * QUARTER + at, COLS)] = gelu(h).astype(jnp.bfloat16)
            return carry

        lax.fori_loop(0, NCOL, body, 0, unroll=True)

    own_rows, their_rows = pl.ds(ROWS, ROWS), pl.ds(0, ROWS)
    loads[2].wait()
    loads[3].wait()
    up_block(own_rows, ROWS, 0)
    for copy in twin_down:
        copy.start()
    loads[4].wait()
    first, second = pl.ds(0, QUARTER), pl.ds(QUARTER, QUARTER)
    for j in range(NCOL):
        cols = pl.ds(j * COLS, COLS)
        own[:, cols] = dot(hidden[own_rows, first], down[first, cols])
    loads[7].start()
    twin_up.wait_recv()
    twin_bias.wait_recv()
    up_block(own_rows, ROWS, 1)
    for copy in row_copies:
        copy.wait_send()
    z_start(0)
    for copy in row_copies:
        copy.wait_recv()
    up_block(their_rows, ROWS, 0)
    up_block(their_rows, ROWS, 1)

    back_copies = []
    for j in range(NCOL):
        twin_down[j].wait_recv()
        cols = pl.ds(j * COLS, COLS)
        back_out[j] = dot(hidden[their_rows, :], down[:, cols]).astype(jnp.bfloat16)
        copy = remote(back_out.at[j], back_in.at[j], S_VBACK + j, partner)
        copy.start()
        back_copies.append(copy)
    pass_on(0)
    for j in range(NCOL):
        cols = pl.ds(j * COLS, COLS)
        own[:, cols] = own[:, cols] + dot(hidden[own_rows, second], down[second, cols])

    remote(
        all_slots.at[pl.ds(0, BLK - 1)], all_slots.at[pl.ds(0, BLK - 1)], S_SLOT, twin
    ).wait()
    loads[5].wait()
    slot_rows = all_slots[:, 0, :]
    my_slots = all_slots[blk]
    count = my_slots.shape[1]
    target = (my_slots >> 7) % BLK
    to_target = lax.broadcasted_iota(jnp.int32, (BLK, count), 0) == target
    rank = jnp.sum(jnp.where(to_target, before(to_target), 0), axis=0, keepdims=True)
    goes = target * CAP + rank
    pick = lax.broadcasted_iota(jnp.int32, (BLK * CAP, count), 0) == goes
    pick = jnp.where(pick, 1.0, 0.0).astype(jnp.bfloat16)

    for_me = (slot_rows >> 7) % BLK == blk
    rank_in = before(for_me)
    position = jnp.where(for_me, (slot_rows & (TOK - 1)) + 1, 0)
    lane = lax.broadcasted_iota(jnp.int32, (BLK, BLK * CAP), 1)
    source = lax.broadcasted_iota(jnp.int32, (BLK, BLK * CAP), 0)
    where = jnp.zeros((BLK, BLK * CAP), jnp.int32)
    for r in range(CAP):
        found = jnp.sum(jnp.where(rank_in == r, position, 0), axis=1, keepdims=True)
        where = where + jnp.where(lane == source * CAP + r, found, 0)
    where = jnp.sum(where, axis=0, keepdims=True) - 1
    placing = lax.broadcasted_iota(jnp.int32, (TOK, BLK * CAP), 0) == where
    placing = jnp.where(placing, 1.0, 0.0)

    for k in range(1, 4):
        o_copy(passing, k).wait_recv()

    @pl.when(odd == 0)
    def _():
        local(passing, slot(0), 8).wait()

    @pl.when(odd == 1)
    def _():
        o_copy(passing, 0).wait_recv()

    pair_o = [remote(slot(k), slot(k), S_PAIR + k, twin) for k in range(4)]
    for copy in pair_o:
        copy.start()

    for j in range(NCOL):
        back_copies[j].wait_recv()
        cols = pl.ds(j * COLS, COLS)
        own[:, cols] = (
            own[:, cols] + back_in[j].astype(jnp.float32) + rows_v[:, cols].astype(jnp.float32)
        )
    z_start(1)
    loads[8].wait()
    for part in range(NROW):
        rows = pl.ds(part * PART, PART)
        normed[rows, :] = normalize(own[rows, :], gain_v[1]).astype(jnp.bfloat16)
    to_row = lax.broadcasted_iota(jnp.int32, (ROWS, ROWS), 0)
    from_row = lax.broadcasted_iota(jnp.int32, (ROWS, ROWS), 1)
    order = from_row == 4 * (to_row & 63) + (to_row >> 6)
    order = jnp.where(order, 1.0, 0.0).astype(jnp.bfloat16)
    for j in range(NCOL):
        moved = dot(order, normed[:, pl.ds(j * COLS, COLS)]).astype(jnp.bfloat16)
        for k in range(4):
            joined[:, pl.ds(k * D + j * COLS, COLS)] = moved[k * 64 : (k + 1) * 64, :]
    loads[7].wait()
    for j in range(NCOL):
        cols = pl.ds(j * COLS, COLS)
        merged[:, cols] = dot(joined[...], proj[:, cols]).astype(jnp.bfloat16)
    spread_rows = dot(pick, merged[...])
    for t in range(BLK):
        send_rows[t] = spread_rows[t * CAP : (t + 1) * CAP, :].astype(jnp.bfloat16)

    def send(i, carry):
        to = (blk + i) % BLK
        remote(send_rows.at[to], got_rows.at[blk], S_A2A, (seq, to)).start()
        return carry

    lax.fori_loop(1, BLK, send, 0)
    got_rows[blk] = send_rows[blk]
    pass_on(1)

    remote(
        send_rows.at[pl.ds(0, BLK - 1)], got_rows.at[pl.ds(0, BLK - 1)], S_A2A, twin
    ).wait()
    for t in range(BLK):
        got_f32[pl.ds(t * CAP, CAP), :] = got_rows[t].astype(jnp.float32)
    loads[6].wait()
    placed = dot(placing.astype(jnp.bfloat16), got_f32[...].astype(jnp.bfloat16))
    filled = jnp.sum(placing, axis=1, keepdims=True) > 0.5
    text_rows[...] = jnp.where(filled, placed, embed_v[...].astype(jnp.float32))

    own_tok = pl.ds(SIDES * TOK, TOK)
    loads[9].wait()
    xt[own_tok, :] = normalize(text_rows[...], gain_v[2]).astype(jnp.bfloat16)
    text_row = [
        remote(xt.at[own_tok], xt.at[pl.ds(i * TOK, TOK)], S_TROW + i, to)
        for i, to in enumerate(sides)
    ]
    for copy in text_row:
        copy.start()

    def text_up_block(part):
        for start, size in ((0, 256), (256, 256), (512, 128)):
            at = pl.ds(part * 4 * SHARD + start, size)
            hidden[:, at] = gelu(dot_t(xt[...], text_w[0, at, :])).astype(jnp.bfloat16)

    theirs = pl.ds(0, SIDES * TOK)
    pair_q = []
    for h in range(2):
        passed_on(h)
        for k in range(4):
            part = half_slot(4 + k, h)
            copy = remote(part, part, S_PAIR + 4 + 4 * h + k, twin)
            copy.start()
            pair_q.append(copy)
    for copy in pair_o:
        copy.wait_recv()
    for copy in text_row:
        copy.wait_recv()
    text_up_block(0)
    for copy in pair_q:
        copy.wait_recv()
    text_up_block(1)
    tback = []
    for j in range(NCOL):
        cols = pl.ds(j * COLS, COLS)
        part = dot(hidden[theirs, first], text_w[1, :, cols]).astype(jnp.bfloat16)
        for i, to in enumerate(sides):
            tback_out[i, j] = part[i * TOK : (i + 1) * TOK, :]
            copy = remote(tback_out.at[i, j], tback_in.at[i, j], S_TBACK + i * NCOL + j, to)
            copy.start()
            tback.append(copy)
    for j in range(NCOL):
        cols = pl.ds(j * COLS, COLS)
        text_rows[:, cols] = text_rows[:, cols] + dot(hidden[own_tok, first], text_w[1, :, cols])
    for j in range(NCOL):
        cols = pl.ds(j * COLS, COLS)
        total = text_rows[:, cols]
        for i in range(SIDES):
            tback[j * SIDES + i].wait_recv()
            total = total + tback_in[i, j].astype(jnp.float32)
        out[:, cols] = total.astype(jnp.bfloat16)

    for h in range(2):
        z_copy(passing, h).wait_send()
    for k in range(1, 4):
        o_copy(passing, k).wait_send()
        for h in range(2):
            q_copy(k, h).wait_send()

    @pl.when(odd == 1)
    def _():
        o_copy(passing, 0).wait_send()
        for h in range(2):
            q_copy(0, h).wait_send()

    for copy in (
        [twin_up, twin_bias]
        + twin_down
        + back_copies
        + pair_o
        + pair_q
        + text_row
        + tback
    ):
        copy.wait_send()


def per_device(
    patches,
    vis_gain,
    vis_up,
    vis_bias,
    vis_down,
    merge_gain,
    merge_proj,
    text_embed,
    slot_index,
    text_gain,
    text_up,
    text_down,
):
    any_ = pl.BlockSpec(memory_space=pl.ANY)
    bf16, f32 = jnp.bfloat16, jnp.float32
    vmem = pltpu.VMEM
    return pl.pallas_call(
        step,
        out_shape=jax.ShapeDtypeStruct(text_embed.shape, bf16),
        in_specs=[any_] * 12,
        out_specs=pl.BlockSpec(memory_space=pltpu.VMEM),
        scratch_shapes=[
            vmem((ROWS, D), bf16),
            vmem((3, 1, D), f32),
            vmem((2, 1, QUARTER), f32),
            vmem((2 * ROWS, D), bf16),
            vmem((2 * ROWS, HALF), bf16),
            vmem((HALF, D), bf16),
            vmem((HALF, D), bf16),
            vmem((4 * D, D), bf16),
            vmem((NCOL, ROWS, COLS), bf16),
            vmem((NCOL, ROWS, COLS), bf16),
            vmem((ROWS, D), f32),
            vmem((ROWS, D), bf16),
            vmem((ROWS // 4, 4 * D), bf16),
            vmem((ROWS // 4, D), bf16),
            vmem((BLK, CAP, D), bf16),
            vmem((BLK, CAP, D), bf16),
            vmem((BLK * CAP, D), f32),
            vmem((BLK, 1, slot_index.shape[0]), jnp.int32),
            vmem((TOK, D), bf16),
            vmem((TOK, D), f32),
            vmem(((SIDES + 1) * TOK, D), bf16),
            vmem((2, QUARTER, D), bf16),
            vmem((SHARD, D), bf16),
            vmem((SIDES, NCOL, TOK, COLS), bf16),
            vmem((SIDES, NCOL, TOK, COLS), bf16),
            pltpu.SemaphoreType.DMA((N_SEM,)),
            pltpu.SemaphoreType.DMA((N_SEM,)),
            pltpu.SemaphoreType.DMA((13,)),
            pltpu.SemaphoreType.REGULAR,
            pltpu.SemaphoreType.REGULAR,
            pltpu.SemaphoreType.REGULAR,
        ],
        compiler_params=pltpu.CompilerParams(
            collective_id=0, has_side_effects=True, vmem_limit_bytes=60 * 2**20
        ),
        name="prefill",
    )(
        patches,
        vis_gain,
        vis_up,
        vis_bias,
        vis_down,
        merge_gain,
        merge_proj,
        text_embed,
        slot_index,
        text_gain,
        text_up,
        text_down,
    )


def solution(mesh):
    placed = (
        P(("seq", "blk"), None),
        P(),
        P("seq", None),
        P("seq"),
        P("seq", None),
        P(),
        P(),
        P(("seq", "blk"), None),
        P(("seq", "blk")),
        P(),
        P("blk", None),
        P("blk", None),
    )
    return jax.shard_map(
        per_device, mesh=mesh, in_specs=placed, out_specs=P(("seq", "blk"), None), check_vma=False
    )
```
